32 devices in a mesh: shard: 8 (over y, x, core), rep: 4 (over z).
Axes of the slice: x: 2, y: 2, z: 4, core: 2. Of those that a mesh axis runs over, the one named last changes fastest.
Arguments:
- tokens: bfloat16 [8, 1024, 2048], P('rep', 'shard'), may hold values from -6 to 6
- lengths: int32 [8], P('rep'), may hold values from 256 to 1024, as said below
- slot_adapter_index: int32 [8], P('rep'), may hold values from 0 to 7
- norm_gain_rows: float32 [2, 2048], replicated, may hold values from 0.1 to 1.9
- norm_shift_rows: float32 [2, 2048], replicated, may hold values from -1.75 to 1.75
- query_key_value_weight: bfloat16 [2048, 6144], P('shard'), may hold values from -0.125 to 0.125
- query_key_value_bias: float32 [6144], replicated, may hold values from -3 to 3
- output_projection_weight: bfloat16 [2048, 2048], P('shard'), may hold values from -0.25 to 0.25
- gate_up_projection: bfloat16 [5632, 2, 2048], P('shard'), may hold values from -0.125 to 0.125
- down_projection_weight: bfloat16 [5632, 2048], P('shard'), may hold values from -0.078125 to 0.078125
- attention_adapter_input: bfloat16 [2048, 384], P('shard'), may hold values from -0.125 to 0.125
- attention_adapter_output: bfloat16 [3, 128, 2048], P(None, None, 'shard'), may hold values from -0.375 to 0.375
- output_adapter_input: bfloat16 [2048, 128], P('shard'), may hold values from -0.125 to 0.125
- output_adapter_output: bfloat16 [128, 2048], P(None, 'shard'), may hold values from -0.375 to 0.375
- feedforward_adapter_input: bfloat16 [2048, 256], P('shard'), may hold values from -0.125 to 0.125
- feedforward_adapter_output: bfloat16 [5632, 2, 128], P('shard'), may hold values from -0.375 to 0.375
- down_adapter_input: bfloat16 [5632, 128], P('shard'), may hold values from -0.078125 to 0.078125
- down_adapter_output: bfloat16 [128, 2048], P(None, 'shard'), may hold values from -0.375 to 0.375
- output_cotangent: bfloat16 [8, 1024, 2048], P('rep', 'shard'), may hold values from -6 to 6
Outputs:
- block_out: bfloat16 [8, 1024, 2048], P('rep', 'shard')
- tokens_grad: float32 [8, 1024, 2048], P('rep', 'shard')
- qkv_lora_a_grad: float32 [2048, 384], P('shard')
- qkv_lora_b_grad: float32 [3, 128, 2048], P(None, None, 'shard')
- out_lora_a_grad: float32 [2048, 128], P('shard')
- out_lora_b_grad: float32 [128, 2048], P(None, 'shard')
- mlp_lora_a_grad: float32 [2048, 256], P('shard')
- mlp_lora_b_grad: float32 [5632, 2, 128], P('shard')
- down_lora_a_grad: float32 [5632, 128], P('shard')
- down_lora_b_grad: float32 [128, 2048], P(None, 'shard')
The draws below stay inside these ranges and needn't reach their ends.
Inputs may be any that keep to these rules, and one draw needn't show every extreme that they name: `lengths`: in every draw some slot holds exactly 1024 tokens and some exactly 256.
All inputs are finite; a program needn't handle non-finite values.
Results may differ from the reference program's by a relative error of at most 0.022.
Values may be sent and summed in bfloat16 or wider, within the bound.
No kernel may reach another device: no remote copies, remote signals or barrier semaphores. Data moves between devices by JAX's collectives and lax.ppermute only.
A program may use at most 448 MiB of HBM per device.

```python
import math
import jax
import jax.numpy as jnp
from jax import lax

MODEL_WIDTH = 2048
HEADS = 32
HEAD_DIM = 64
ROT = 16
HIDDEN_UNITS = 5632
ADAPTER_COUNT = 8
ADAPTER_RANK = 16
SEQ = 1024
MIN_LEN = 256
SLOTS = 8


def draw_lengths(key, part):
    first_key, second_key = jax.random.split(key)
    lengths_drawn = jax.random.randint(first_key, (SLOTS,), MIN_LEN, SEQ + 1, dtype=jnp.int32)
    shuffled = jax.random.permutation(second_key, SLOTS)
    lengths_drawn = lengths_drawn.at[shuffled[0]].set(SEQ)
    return lengths_drawn.at[shuffled[1]].set(MIN_LEN)


def place_ends(array, key, smallest, largest):
    longest = array.shape.index(max(array.shape))
    spots = []
    for shift in (0, 1):
        where = [jax.random.randint(jax.random.fold_in(key, axis), (), 0, length) for axis, length in enumerate(array.shape)]
        where[longest] = (where[longest] + shift) % array.shape[longest]
        spots.append(tuple(where))
    return array.at[spots[0]].set(smallest).at[spots[1]].set(largest)


def level_of(stream_key, dims, pieces, least, top_value):
    gain = 1.0
    for position, shards_of in pieces:
        heights = jax.random.uniform(jax.random.fold_in(jax.random.fold_in(stream_key, 6), position), (shards_of,), jnp.float32, least / len(pieces), top_value / len(pieces))
        gain = gain * jnp.repeat(jnp.exp(heights), dims[position] // shards_of).reshape((-1,) + (1,) * (len(dims) - 1 - position))
    return gain


def noise(stream_key, dims, deviation, limit, pieces=(), kind=jnp.bfloat16):
    gain = level_of(stream_key, dims, pieces, -0.22, 0.18) if pieces else 1.0
    values = jax.random.normal(stream_key, dims, jnp.float32) * deviation * gain
    return jnp.minimum(jnp.maximum(values, -limit), limit).astype(kind)


def setup_inputs(seed: int = 0) -> dict:
    seeds = jax.random.split(jax.random.key(seed), 20)
    return {
        "tokens": noise(seeds[0], (SLOTS, SEQ, MODEL_WIDTH), 1.0, 6.0, ((0, 4), (1, 8))),
        "lengths": draw_lengths(jax.random.fold_in(seeds[19], 71), 0),
        "slot_adapter_index": place_ends(jax.random.randint(seeds[2], (SLOTS,), 0, ADAPTER_COUNT), jax.random.fold_in(seeds[2], 1), 0, ADAPTER_COUNT - 1).astype(jnp.int32),
        "norm_gain_rows": jnp.clip(1.0 + 0.18 * jax.random.normal(seeds[3], (2, MODEL_WIDTH), jnp.float32), 0.1, 1.9),
        "norm_shift_rows": noise(seeds[4], (2, MODEL_WIDTH), 0.3, 1.75, (), jnp.float32),
        "query_key_value_weight": noise(seeds[5], (MODEL_WIDTH, 3 * MODEL_WIDTH), MODEL_WIDTH ** -0.5, 0.125, ((0, 8),)),
        "query_key_value_bias": noise(seeds[6], (3 * MODEL_WIDTH,), 0.5, 3.0, (), jnp.float32),
        "output_projection_weight": noise(seeds[7], (MODEL_WIDTH, MODEL_WIDTH), (MODEL_WIDTH // 4) ** -0.5, 0.25, ((0, 8),)),
        "gate_up_projection": noise(seeds[8], (HIDDEN_UNITS, 2, MODEL_WIDTH), MODEL_WIDTH ** -0.5, 0.125, ((0, 8),)),
        "down_projection_weight": noise(seeds[9], (HIDDEN_UNITS, MODEL_WIDTH), HIDDEN_UNITS ** -0.5, 0.078125, ((0, 8),)),
        "attention_adapter_input": noise(seeds[10], (MODEL_WIDTH, 3 * ADAPTER_COUNT * ADAPTER_RANK), MODEL_WIDTH ** -0.5, 0.125, ((0, 8),)),
        "attention_adapter_output": noise(seeds[11], (3, ADAPTER_COUNT * ADAPTER_RANK, MODEL_WIDTH), (16 * ADAPTER_RANK) ** -0.5, 0.375, ((2, 8),)),
        "output_adapter_input": noise(seeds[12], (MODEL_WIDTH, ADAPTER_COUNT * ADAPTER_RANK), MODEL_WIDTH ** -0.5, 0.125, ((0, 8),)),
        "output_adapter_output": noise(seeds[13], (ADAPTER_COUNT * ADAPTER_RANK, MODEL_WIDTH), (16 * ADAPTER_RANK) ** -0.5, 0.375, ((1, 8),)),
        "feedforward_adapter_input": noise(seeds[14], (MODEL_WIDTH, 2 * ADAPTER_COUNT * ADAPTER_RANK), MODEL_WIDTH ** -0.5, 0.125, ((0, 8),)),
        "feedforward_adapter_output": noise(seeds[15], (HIDDEN_UNITS, 2, ADAPTER_COUNT * ADAPTER_RANK), (16 * ADAPTER_RANK) ** -0.5, 0.375, ((0, 8),)),
        "down_adapter_input": noise(seeds[16], (HIDDEN_UNITS, ADAPTER_COUNT * ADAPTER_RANK), HIDDEN_UNITS ** -0.5, 0.078125, ((0, 8),)),
        "down_adapter_output": noise(seeds[17], (ADAPTER_COUNT * ADAPTER_RANK, MODEL_WIDTH), (16 * ADAPTER_RANK) ** -0.5, 0.375, ((1, 8),)),
        "output_cotangent": noise(seeds[18], (SLOTS, SEQ, MODEL_WIDTH), 1.0, 6.0, ((0, 4), (1, 8))),
    }


@jax.custom_vjp
def low(v):
    return lax.optimization_barrier(v.astype(jnp.bfloat16)).astype(jnp.float32)

@jax.custom_vjp
def reduced_backward(v):
    return v

def low_keep(v):
    return (low(v), None)

def low_pass(kept, grad):
    return (grad,)

def back_keep(v):
    return (v, None)

def back_low(kept, grad):
    return (low(grad),)
low.defvjp(low_keep, low_pass)
reduced_backward.defvjp(back_keep, back_low)
highest_precision = lax.Precision.HIGHEST
adapter_scale = 2.0
norm_epsilon = 1e-05
rotary_base = 10000.0
masked_score = -1e+30

def layer_norm(values, gain_row, shift_row):
    average = lax.optimization_barrier(jnp.mean(values, axis=-1, keepdims=True))
    centered = values - average
    variance = lax.optimization_barrier(jnp.mean(centered * centered, axis=-1, keepdims=True))
    return centered * lax.rsqrt(variance + norm_epsilon) * gain_row + shift_row

def rotary_tables(places):
    half_rot = ROT // 2
    spacing = jnp.arange(half_rot, dtype=jnp.float32) * (-2.0 * math.log(rotary_base) / ROT)
    turn_angles = places.astype(jnp.float32)[:, None] * jnp.exp(spacing)[None, :]
    return (jnp.cos(turn_angles), jnp.sin(turn_angles))

def rotate(values, cosine_table, sine_table):
    half_rot = ROT // 2
    former = values[..., :half_rot]
    latter = values[..., half_rot:ROT]
    cos_rows = cosine_table[:, None, :]
    sin_rows = sine_table[:, None, :]
    return jnp.concatenate([former * cos_rows - latter * sin_rows, latter * cos_rows + former * sin_rows, values[..., ROT:]], axis=-1)

def adapter_slice(layer_inputs, down_mat, up_mat, select_adapter_rows, part_count, pattern):
    row_count = layer_inputs.shape[0]
    middle = jnp.dot(layer_inputs, down_mat, precision=highest_precision).reshape(row_count, part_count, ADAPTER_COUNT * ADAPTER_RANK)
    middle = low(reduced_backward(middle * select_adapter_rows[:, None, :]))
    return jnp.einsum(pattern, middle, up_mat, precision=highest_precision)

def attend(queries, keys_all, values_all, lengths_here):
    slot_count = queries.shape[0]
    block_rows = min(512, SEQ)
    block_count = SEQ // block_rows
    score_scale = HEAD_DIM ** (-0.5)
    key_places = jnp.arange(SEQ, dtype=jnp.int32)
    stacked = jnp.moveaxis(queries.reshape(slot_count, block_count, block_rows, HEADS, HEAD_DIM), 1, 0)
    starts = jnp.arange(block_count, dtype=jnp.int32) * block_rows

    def one_block(operands):
        query_block, first_row = operands
        query_places = first_row + jnp.arange(block_rows, dtype=jnp.int32)
        scores = reduced_backward(jnp.einsum('gqhd,gkhd->gqhk', query_block, keys_all, precision=highest_precision) * score_scale)
        allowed = (key_places[None, None, None, :] <= query_places[None, :, None, None]) & (key_places[None, None, None, :] < lengths_here[:, None, None, None])
        scores = jnp.where(allowed, scores, masked_score)
        shifted = jnp.exp(scores - lax.optimization_barrier(jnp.max(scores, axis=-1, keepdims=True)))
        probabilities = shifted / lax.optimization_barrier(jnp.sum(shifted, axis=-1, keepdims=True))
        return jnp.einsum('gqhk,gkhd->gqhd', low(probabilities), values_all, precision=highest_precision)
    outputs = lax.map(jax.checkpoint(one_block), (stacked, starts))
    return jnp.moveaxis(outputs, 0, 1).reshape(slot_count, SEQ, HEADS * HEAD_DIM)

def forward(tokens_in, adapter_tables, frozen, lengths_here, ids_here):
    attention_input_map, attention_output_map, output_input_map, output_output_map, feedforward_input_map, feedforward_output_map, down_input_map, down_output_map = adapter_tables
    gains, shifts, qkv_full, qkv_shift, output_complete, gate_full, down_complete = frozen
    slot_count = tokens_in.shape[0]
    row_count = slot_count * SEQ
    places = jnp.arange(SEQ, dtype=jnp.int32)
    valid_rows = (places[None, :] < lengths_here[:, None]).astype(jnp.float32).reshape(row_count, 1)
    columns = ADAPTER_COUNT * ADAPTER_RANK
    choose = (jnp.arange(columns, dtype=jnp.int32)[None, :] // ADAPTER_RANK == ids_here[:, None]).astype(jnp.float32)
    select_adapter_rows = jnp.broadcast_to(choose[:, None, :], (slot_count, SEQ, columns)).reshape(row_count, columns)
    flat_rows = tokens_in.reshape(row_count, MODEL_WIDTH)
    first_normalized = low(layer_norm(flat_rows, gains[0], shifts[0]))
    projected_rows = jnp.dot(first_normalized, qkv_full, precision=highest_precision).reshape(row_count, 3, MODEL_WIDTH) + qkv_shift.reshape(3, MODEL_WIDTH)
    projected_rows = reduced_backward(projected_rows + adapter_scale * adapter_slice(first_normalized, attention_input_map, attention_output_map, select_adapter_rows, 3, 'wsq,sql->wsl'))
    cosine_table, sine_table = rotary_tables(places)
    shaped = projected_rows.reshape(slot_count, SEQ, 3, HEADS, HEAD_DIM)
    queries = low(rotate(shaped[:, :, 0], cosine_table, sine_table))
    keys_all = low(rotate(shaped[:, :, 1], cosine_table, sine_table))
    values_all = low(shaped[:, :, 2])
    attention_output = low(reduced_backward(attend(queries, keys_all, values_all, lengths_here).reshape(row_count, MODEL_WIDTH)))
    residual_branch = jnp.dot(attention_output, output_complete, precision=highest_precision) + adapter_scale * adapter_slice(attention_output, output_input_map, output_output_map[None], select_adapter_rows, 1, 'wsq,sql->wsl')[:, 0]
    hidden_input_rows = flat_rows + reduced_backward(residual_branch)
    second_normalized = low(layer_norm(hidden_input_rows, gains[1], shifts[1]))
    gate_up_hidden = jnp.einsum('td,fjd->tjf', second_normalized, gate_full, precision=highest_precision)
    gate_up_hidden = reduced_backward(gate_up_hidden + adapter_scale * adapter_slice(second_normalized, feedforward_input_map, feedforward_output_map, select_adapter_rows, 2, 'ilz,plz->ilp'))
    gated_hidden = low(jax.nn.silu(gate_up_hidden[:, 0]) * gate_up_hidden[:, 1])
    feedforward_output = jnp.dot(gated_hidden, down_complete, precision=highest_precision) + adapter_scale * adapter_slice(gated_hidden, down_input_map, down_output_map[None], select_adapter_rows, 1, 'wsq,sql->wsl')[:, 0]
    return ((hidden_input_rows + reduced_backward(feedforward_output)) * valid_rows).reshape(slot_count, SEQ, MODEL_WIDTH)

def reference(tokens, lengths, slot_adapter_index, norm_gain_rows, norm_shift_rows, query_key_value_weight, query_key_value_bias, output_projection_weight, gate_up_projection, down_projection_weight, attention_adapter_input, attention_adapter_output, output_adapter_input, output_adapter_output, feedforward_adapter_input, feedforward_adapter_output, down_adapter_input, down_adapter_output, output_cotangent):
    frozen = (norm_gain_rows.astype(jnp.float32), norm_shift_rows.astype(jnp.float32), query_key_value_weight.astype(jnp.float32), query_key_value_bias.astype(jnp.float32), output_projection_weight.astype(jnp.float32), gate_up_projection.astype(jnp.float32), down_projection_weight.astype(jnp.float32))
    adapter_tables = (attention_adapter_input.astype(jnp.float32), attention_adapter_output.astype(jnp.float32), output_adapter_input.astype(jnp.float32), output_adapter_output.astype(jnp.float32), feedforward_adapter_input.astype(jnp.float32), feedforward_adapter_output.astype(jnp.float32), down_adapter_input.astype(jnp.float32), down_adapter_output.astype(jnp.float32))
    per_step = math.gcd(SLOTS, 2)
    step_count = SLOTS // per_step

    def one_step(totals, step_index):
        first_slot = (step_index * per_step).astype(jnp.int32)
        tokens_in = lax.dynamic_slice_in_dim(tokens, first_slot, per_step, 0).astype(jnp.float32)
        lengths_here = lax.dynamic_slice_in_dim(lengths, first_slot, per_step, 0)
        ids_here = lax.dynamic_slice_in_dim(slot_adapter_index, first_slot, per_step, 0)
        cotangent = lax.dynamic_slice_in_dim(output_cotangent, first_slot, per_step, 0).astype(jnp.float32)

        def layer_call(layer_inputs, params):
            return forward(layer_inputs, params, frozen, lengths_here, ids_here)
        result, pullback = jax.vjp(layer_call, tokens_in, adapter_tables)
        input_grad, param_grads = pullback(cotangent)
        totals = jax.tree.map(jnp.add, totals, param_grads)
        return (totals, (result.astype(jnp.bfloat16), input_grad))
    initial = jax.tree.map(jnp.zeros_like, adapter_tables)
    totals, (results, input_grads) = lax.scan(one_step, initial, jnp.arange(step_count, dtype=jnp.int32))
    return (results.reshape(SLOTS, SEQ, MODEL_WIDTH), input_grads.reshape(SLOTS, SEQ, MODEL_WIDTH), totals[0], totals[1], totals[2], totals[3], totals[4], totals[5], totals[6], totals[7])
```

```python
import math

import jax
import jax.numpy as jnp
from jax import lax
from jax.sharding import PartitionSpec as P

HEAD_DIM = 64
ROT = 16
ADAPTER_COUNT = 8
RANK = 16
EXTRA = 128

adapter_scale = 2.0
norm_epsilon = 1e-05
rotary_base = 10000.0
masked_score = -1e30
low = jnp.bfloat16


def dot(a, b):
    return jnp.dot(a, b, preferred_element_type=jnp.float32)


def dot_nt(a, b):
    return lax.dot_general(a, b, (((1,), (1,)), ((), ())), preferred_element_type=jnp.float32)


def dot_tn(a, b):
    return lax.dot_general(a, b, (((0,), (0,)), ((), ())), preferred_element_type=jnp.float32)


def layer_norm(values, gain_row, shift_row):
    average = jnp.mean(values, axis=-1, keepdims=True)
    centered = values - average
    variance = jnp.mean(centered * centered, axis=-1, keepdims=True)
    inverse = lax.rsqrt(variance + norm_epsilon)
    unit_rows = centered * inverse
    return (unit_rows * gain_row + shift_row, unit_rows, inverse)


def layer_norm_back(grad_rows, unit_rows, inverse, gain_row):
    scaled = grad_rows * gain_row
    return inverse * (
        scaled
        - jnp.mean(scaled, axis=-1, keepdims=True)
        - unit_rows * jnp.mean(scaled * unit_rows, axis=-1, keepdims=True)
    )


def rotary_tables(span, heads_here):
    half_rot = ROT // 2
    lane = jnp.arange(heads_here * HEAD_DIM, dtype=jnp.int32) % HEAD_DIM
    turn = (lane % half_rot).astype(jnp.float32) * (-2.0 * math.log(rotary_base) / ROT)
    places = jnp.arange(span, dtype=jnp.int32).astype(jnp.float32)
    angles = places[:, None] * jnp.exp(turn)[None, :]
    cosine = jnp.where(lane[None, :] < ROT, jnp.cos(angles), 1.0)
    sine = jnp.sin(angles)
    sine_former = jnp.where(lane[None, :] < half_rot, -sine, 0.0)
    sine_latter = jnp.where((lane[None, :] >= half_rot) & (lane[None, :] < ROT), sine, 0.0)
    return (cosine, sine_former, sine_latter)


def turn_rows(values, tables):
    cosine, sine_former, sine_latter = tables
    half_rot = ROT // 2
    return (
        values * cosine
        + jnp.roll(values, -half_rot, axis=1) * sine_former
        + jnp.roll(values, half_rot, axis=1) * sine_latter
    )


def unturn_rows(grads, tables):
    cosine, sine_former, sine_latter = tables
    half_rot = ROT // 2
    return (
        grads * cosine
        + jnp.roll(grads * sine_former, half_rot, axis=1)
        + jnp.roll(grads * sine_latter, -half_rot, axis=1)
    )


def head_split(rows):
    return rows.reshape(rows.shape[0], -1, HEAD_DIM)


def attend(queries, keys, values, length):
    span = queries.shape[0]
    places = jnp.arange(span, dtype=jnp.int32)
    allowed = (places[None, :] <= places[:, None]) & (places[None, :] < length)
    scores = jnp.einsum(
        "qgd,kgd->gqk", head_split(queries), head_split(keys), preferred_element_type=jnp.float32
    ) * (HEAD_DIM**-0.5)
    scores = jnp.where(allowed[None], scores, masked_score)
    top = jnp.max(scores, axis=-1, keepdims=True)
    shifted = jnp.exp(scores - top)
    total = jnp.sum(shifted, axis=-1, keepdims=True)
    probabilities = shifted / total
    attended = jnp.einsum(
        "gqk,kgd->qgd",
        probabilities.astype(low),
        head_split(values),
        preferred_element_type=jnp.float32,
    )
    return (attended.reshape(span, -1), top + jnp.log(total))


def attend_back(queries, keys, values, lse, attended, grads, length):
    span = queries.shape[0]
    places = jnp.arange(span, dtype=jnp.int32)
    allowed = (places[None, :] <= places[:, None]) & (places[None, :] < length)
    q, k, v, g = (head_split(rows) for rows in (queries, keys, values, grads))
    delta = jnp.sum(g.astype(jnp.float32) * head_split(attended), axis=-1).T[:, :, None]
    scale = HEAD_DIM**-0.5
    scores = jnp.einsum("qgd,kgd->gqk", q, k, preferred_element_type=jnp.float32) * scale
    probabilities = jnp.where(allowed[None], jnp.exp(scores - lse), 0.0)
    prob_grad = jnp.einsum("qgd,kgd->gqk", g, v, preferred_element_type=jnp.float32)
    score_grad = (probabilities * (prob_grad - delta)).astype(low)
    q_grad = scale * jnp.einsum("gqk,kgd->qgd", score_grad, k, preferred_element_type=jnp.float32)
    k_grad = scale * jnp.einsum("gqk,qgd->kgd", score_grad, q, preferred_element_type=jnp.float32)
    v_grad = jnp.einsum(
        "gqk,qgd->kgd", probabilities.astype(low), g, preferred_element_type=jnp.float32
    )
    return tuple(rows.reshape(span, -1) for rows in (q_grad, k_grad, v_grad))


def pick_columns(table, adapter, blocks):
    width = ADAPTER_COUNT * RANK
    return jnp.concatenate(
        [
            lax.dynamic_slice_in_dim(table[:, j * width : (j + 1) * width], adapter * RANK, RANK, 1)
            for j in range(blocks)
        ],
        axis=1,
    )


def widen(*parts):
    rows = parts[0].shape[0]
    used = sum(part.shape[1] for part in parts[1:])
    return jnp.concatenate([*parts, jnp.zeros((rows, EXTRA - used), parts[0].dtype)], axis=1)


def gather_rows(rows):
    return lax.all_gather(rows, "shard", axis=0, tiled=True)


def scatter_rows(rows):
    return lax.psum_scatter(rows, "shard", scatter_dimension=0, tiled=True)


def per_device(
    tokens,
    lengths,
    slot_adapter_index,
    norm_gain_rows,
    norm_shift_rows,
    query_key_value_weight,
    query_key_value_bias,
    output_projection_weight,
    gate_up_projection,
    down_projection_weight,
    attention_adapter_input,
    attention_adapter_output,
    output_adapter_input,
    output_adapter_output,
    feedforward_adapter_input,
    feedforward_adapter_output,
    down_adapter_input,
    down_adapter_output,
    output_cotangent,
):
    slot_count, local_span, width = tokens.shape
    shards = lax.axis_size("shard")
    reps = lax.axis_size("rep")
    me = lax.axis_index("shard")
    span = local_span * shards
    own = width // shards
    hidden = gate_up_projection.shape[0]
    places = me * local_span + jnp.arange(local_span, dtype=jnp.int32)
    slots = range(slot_count)
    adapters = [slot_adapter_index[s] for s in slots]

    map_pieces = []
    for s in slots:
        a = adapters[s]
        rows_of = lambda table: lax.dynamic_slice_in_dim(table, a * RANK, RANK, 0).T
        map_pieces += [
            pick_columns(attention_adapter_input, a, 3),
            pick_columns(feedforward_adapter_input, a, 2),
            pick_columns(output_adapter_input, a, 1),
            rows_of(output_adapter_output),
            rows_of(down_adapter_output),
        ]
    maps = gather_rows(jnp.concatenate(map_pieces, axis=1)).reshape(width, slot_count, -1)

    weight_here = lax.all_to_all(
        query_key_value_weight.reshape(own, 3, shards, own), "shard", 2, 0, tiled=True
    ).reshape(width, 3 * own)
    bias_here = lax.dynamic_slice_in_dim(
        query_key_value_bias.reshape(3, width), me * own, own, 1
    ).reshape(1, 3 * own)
    output_full = gather_rows(output_projection_weight)
    tables = rotary_tables(span, own // HEAD_DIM)
    gate_up = gate_up_projection.reshape(hidden * 2, width)
    gate_weight = gate_up_projection[:, 0]
    up_weight = gate_up_projection[:, 1]

    kept = []
    for s in slots:
        a = adapters[s]
        own_maps = maps[:, s]
        qkv_in, mlp_in = (own_maps[:, :48], own_maps[:, 48:80])
        out_in, out_out, down_out = (own_maps[:, 80:96], own_maps[:, 96:112], own_maps[:, 112:128])
        valid = (places < lengths[s]).astype(jnp.float32)[:, None]
        inputs = tokens[s].astype(jnp.float32)
        grad_rows = output_cotangent[s].astype(jnp.float32) * valid
        grad_low = grad_rows.astype(low)
        down_mid_grad = (adapter_scale * dot(grad_low, down_out)).astype(low)
        normed, unit_one, inverse_one = layer_norm(inputs, norm_gain_rows[0], norm_shift_rows[0])
        normed = normed.astype(low)
        qkv_mid = dot(normed, qkv_in).astype(low)
        kept.append(
            dict(
                a=a,
                qkv_in=qkv_in,
                mlp_in=mlp_in,
                out_in=out_in,
                out_out=out_out,
                down_out=down_out,
                valid=valid,
                inputs=inputs,
                grad_rows=grad_rows,
                grad_low=grad_low,
                down_mid_grad=down_mid_grad,
                normed=normed,
                unit_one=unit_one,
                inverse_one=inverse_one,
                qkv_mid=qkv_mid,
                qkv_out=lax.dynamic_slice_in_dim(attention_adapter_output, a * RANK, RANK, 1),
                mlp_out=lax.dynamic_slice_in_dim(feedforward_adapter_output, a * RANK, RANK, 2),
                down_in=lax.dynamic_slice_in_dim(down_adapter_input, a * RANK, RANK, 1),
            )
        )

    for s in slots:
        k = kept[s]
        wide = gather_rows(widen(k["normed"], k["qkv_mid"]))
        k["all_mid"] = wide[:, width : width + 3 * RANK]
        projected = dot(wide[:, :width], weight_here) + bias_here
        update = jnp.concatenate(
            [
                dot(k["all_mid"][:, j * RANK : (j + 1) * RANK], k["qkv_out"][j])
                for j in range(3)
            ],
            axis=1,
        )
        projected = projected + adapter_scale * update
        k["q"] = turn_rows(projected[:, :own], tables).astype(low)
        k["k"] = turn_rows(projected[:, own : 2 * own], tables).astype(low)
        k["v"] = projected[:, 2 * own :].astype(low)
        k["attended"], k["lse"] = attend(k["q"], k["k"], k["v"], lengths[s])

    for s in slots:
        k = kept[s]
        attended = lax.all_to_all(k["attended"].astype(low), "shard", 0, 1, tiled=True)
        out_mid = dot(attended, k["out_in"]).astype(low)
        hidden_in = k["inputs"] + (
            dot(attended, output_full) + adapter_scale * dot_nt(out_mid, k["out_out"])
        )
        normed_two, unit_two, inverse_two = layer_norm(
            hidden_in, norm_gain_rows[1], norm_shift_rows[1]
        )
        normed_two = normed_two.astype(low)
        mlp_mid = dot(normed_two, k["mlp_in"]).astype(low)
        k.update(
            attended_rows=attended,
            out_mid=out_mid,
            hidden_in=hidden_in,
            normed_two=normed_two,
            unit_two=unit_two,
            inverse_two=inverse_two,
            mlp_mid=mlp_mid,
        )

    for s in slots:
        k = kept[s]
        wide = gather_rows(widen(k["normed_two"], k["mlp_mid"]))
        grad_wide = gather_rows(widen(k["grad_low"], k["down_mid_grad"]))
        two, mids = (wide[:, :width], wide[:, width : width + 2 * RANK])
        parts = []
        for j, weight in enumerate((gate_weight, up_weight)):
            mid = mids[:, j * RANK : (j + 1) * RANK]
            parts.append(
                dot_nt(two, weight) + adapter_scale * dot_nt(mid, k["mlp_out"][:, j])
            )
        gate, up = parts
        sigmoid = jax.nn.sigmoid(gate)
        silu = gate * sigmoid
        activated = (silu * up).astype(low)
        down_partial = jnp.concatenate(
            [
                dot(activated, down_projection_weight).astype(low),
                dot(activated, k["down_in"]).astype(low),
                jnp.zeros((span, EXTRA - RANK), low),
            ],
            axis=1,
        )
        down_mid_grad = grad_wide[:, width : width + RANK]
        hidden_grad = dot_nt(grad_wide[:, :width], down_projection_weight) + dot_nt(
            down_mid_grad, k["down_in"]
        )
        gate_grad = (hidden_grad * up * sigmoid * (1.0 + gate * (1.0 - sigmoid))).astype(low)
        up_grad = (hidden_grad * silu).astype(low)
        two_partial = jnp.concatenate(
            [
                (dot(gate_grad, gate_weight) + dot(up_grad, up_weight)).astype(low),
                (adapter_scale * dot(gate_grad, k["mlp_out"][:, 0])).astype(low),
                (adapter_scale * dot(up_grad, k["mlp_out"][:, 1])).astype(low),
                jnp.zeros((span, EXTRA - 2 * RANK), low),
            ],
            axis=1,
        )
        k["two_sum"] = scatter_rows(two_partial)
        k["down_sum"] = scatter_rows(down_partial)
        k["down_a"] = dot_tn(activated, down_mid_grad)
        k["mlp_b"] = adapter_scale * jnp.concatenate(
            [dot_tn(gate_grad, mids[:, :RANK]), dot_tn(up_grad, mids[:, RANK:])], axis=1
        )

    for s in slots:
        k = kept[s]
        mlp_mid_grad = k["two_sum"][:, width : width + 2 * RANK]
        two_grad = k["two_sum"][:, :width].astype(jnp.float32) + dot_nt(mlp_mid_grad, k["mlp_in"])
        residual_grad = k["grad_rows"] + layer_norm_back(
            two_grad, k["unit_two"], k["inverse_two"], norm_gain_rows[1]
        )
        branch = residual_grad.astype(low)
        out_mid_grad = (adapter_scale * dot(branch, k["out_out"])).astype(low)
        attended_grad = (dot_nt(branch, output_full) + dot_nt(out_mid_grad, k["out_in"])).astype(
            low
        )
        k.update(
            residual_grad=residual_grad,
            branch=branch,
            mlp_mid_grad=mlp_mid_grad,
            out_mid_grad=out_mid_grad,
        )
        k["head_grad"] = lax.all_to_all(attended_grad, "shard", 1, 0, tiled=True)

    for s in slots:
        k = kept[s]
        q_grad, k_grad, v_grad = attend_back(
            k["q"], k["k"], k["v"], k["lse"], k["attended"], k["head_grad"], lengths[s]
        )
        projected_grad = jnp.concatenate(
            [unturn_rows(q_grad, tables), unturn_rows(k_grad, tables), v_grad], axis=1
        ).astype(low)
        mid_parts = []
        b_parts = []
        for j in range(3):
            part = projected_grad[:, j * own : (j + 1) * own]
            mid_parts.append((adapter_scale * dot_nt(part, k["qkv_out"][j])).astype(low))
            b_parts.append(
                adapter_scale * dot_tn(k["all_mid"][:, j * RANK : (j + 1) * RANK], part)
            )
        k["qkv_b"] = jnp.stack(b_parts)
        k["one_sum"] = scatter_rows(
            jnp.concatenate(
                [
                    dot_nt(projected_grad, weight_here).astype(low),
                    *mid_parts,
                    jnp.zeros((span, EXTRA - 3 * RANK), low),
                ],
                axis=1,
            )
        )

    block_parts = []
    token_parts = []
    compact = []
    for s in slots:
        k = kept[s]
        down_mid = k["down_sum"][:, width : width + RANK]
        feed = k["down_sum"][:, :width].astype(jnp.float32) + adapter_scale * dot_nt(
            down_mid, k["down_out"]
        )
        block_parts.append(((k["hidden_in"] + feed) * k["valid"]).astype(low))
        mid_grad = k["one_sum"][:, width : width + 3 * RANK]
        normed_grad = k["one_sum"][:, :width].astype(jnp.float32) + dot_nt(mid_grad, k["qkv_in"])
        token_parts.append(
            k["residual_grad"]
            + layer_norm_back(normed_grad, k["unit_one"], k["inverse_one"], norm_gain_rows[0])
        )
        compact += [
            dot_tn(k["normed"], mid_grad),
            dot_tn(k["normed_two"], k["mlp_mid_grad"]),
            dot_tn(k["attended_rows"], k["out_mid_grad"]),
            adapter_scale * dot_tn(k["branch"], k["out_mid"]),
            adapter_scale * dot_tn(k["grad_low"], down_mid),
        ]
    owned = scatter_rows(jnp.concatenate(compact, axis=1).astype(low))

    owned = owned.reshape(own, slot_count, 8, RANK)
    grads = []
    for s in slots:
        k = kept[s]
        part = [owned[:, s, j] for j in range(8)]
        part += [k["qkv_b"][j].T.astype(low) for j in range(3)]
        part += [k["mlp_b"][:, :RANK].astype(low), k["mlp_b"][:, RANK:].astype(low)]
        part += [k["down_a"].astype(low)]
        grads.append(jnp.concatenate(part, axis=0))
    shared = lax.all_gather(jnp.stack(grads), "rep", axis=0, tiled=True)
    index = lax.all_gather(slot_adapter_index, "rep", axis=0, tiled=True)
    spread = (index[:, None] == jnp.arange(ADAPTER_COUNT, dtype=jnp.int32)[None, :]).astype(
        jnp.float32
    )
    full = jnp.einsum(
        "nxr,na->xar", shared.astype(jnp.float32), spread, precision=lax.Precision.HIGHEST
    ).reshape(shared.shape[1], ADAPTER_COUNT * RANK)
    pieces = [full[j * own : (j + 1) * own] for j in range(11)]
    rest = full[11 * own :].reshape(3, hidden, ADAPTER_COUNT * RANK)
    return (
        jnp.stack(block_parts),
        jnp.stack(token_parts),
        jnp.concatenate(pieces[:3], axis=1),
        jnp.stack([piece.T for piece in pieces[8:11]]),
        pieces[5],
        pieces[6].T,
        jnp.concatenate(pieces[3:5], axis=1),
        jnp.stack([rest[0], rest[1]], axis=1),
        rest[2],
        pieces[7].T,
    )


def solution(mesh):
    rows = P("shard", None)
    in_specs = (
        P("rep", "shard", None),
        P("rep"),
        P("rep"),
        P(),
        P(),
        rows,
        P(),
        rows,
        P("shard", None, None),
        rows,
        rows,
        P(None, None, "shard"),
        rows,
        P(None, "shard"),
        rows,
        P("shard", None, None),
        rows,
        P(None, "shard"),
        P("rep", "shard", None),
    )
    out_specs = (
        P("rep", "shard", None),
        P("rep", "shard", None),
        rows,
        P(None, None, "shard"),
        rows,
        P(None, "shard"),
        rows,
        P("shard", None, None),
        rows,
        P(None, "shard"),
    )
    return jax.shard_map(
        per_device, mesh=mesh, in_specs=in_specs, out_specs=out_specs, check_vma=False
    )
```

```python
import math

import jax
import jax.numpy as jnp
from jax import lax
from jax.experimental import pallas as pl
from jax.experimental.pallas import tpu as pltpu
from jax.sharding import PartitionSpec as P

HEAD_DIM = 64
ROT = 16
ADAPTER_COUNT = 8
RANK = 16
EXTRA = 128

adapter_scale = 2.0
norm_epsilon = 1e-05
rotary_base = 10000.0
masked_score = -1e30
low = jnp.bfloat16


def dot(a, b):
    return jnp.dot(a, b, preferred_element_type=jnp.float32)


def dot_nt(a, b):
    return lax.dot_general(a, b, (((1,), (1,)), ((), ())), preferred_element_type=jnp.float32)


def dot_tn(a, b):
    return lax.dot_general(a, b, (((0,), (0,)), ((), ())), preferred_element_type=jnp.float32)


def layer_norm(values, gain_row, shift_row):
    average = jnp.mean(values, axis=-1, keepdims=True)
    centered = values - average
    variance = jnp.mean(centered * centered, axis=-1, keepdims=True)
    inverse = lax.rsqrt(variance + norm_epsilon)
    unit_rows = centered * inverse
    return (unit_rows * gain_row + shift_row, unit_rows, inverse)


def layer_norm_back(grad_rows, unit_rows, inverse, gain_row):
    scaled = grad_rows * gain_row
    return inverse * (
        scaled
        - jnp.mean(scaled, axis=-1, keepdims=True)
        - unit_rows * jnp.mean(scaled * unit_rows, axis=-1, keepdims=True)
    )


def rotary_tables(span, heads_here):
    half_rot = ROT // 2
    lane = jnp.arange(heads_here * HEAD_DIM, dtype=jnp.int32) % HEAD_DIM
    turn = (lane % half_rot).astype(jnp.float32) * (-2.0 * math.log(rotary_base) / ROT)
    places = jnp.arange(span, dtype=jnp.int32).astype(jnp.float32)
    angles = places[:, None] * jnp.exp(turn)[None, :]
    cosine = jnp.where(lane[None, :] < ROT, jnp.cos(angles), 1.0)
    sine = jnp.sin(angles)
    sine_former = jnp.where(lane[None, :] < half_rot, -sine, 0.0)
    sine_latter = jnp.where((lane[None, :] >= half_rot) & (lane[None, :] < ROT), sine, 0.0)
    return (cosine, sine_former, sine_latter)


def turn_rows(values, tables):
    cosine, sine_former, sine_latter = tables
    half_rot = ROT // 2
    lanes = values.shape[1]
    return (
        values * cosine
        + pltpu.roll(values, lanes - half_rot, 1) * sine_former
        + pltpu.roll(values, half_rot, 1) * sine_latter
    )


def unturn_rows(grads, tables):
    cosine, sine_former, sine_latter = tables
    half_rot = ROT // 2
    lanes = grads.shape[1]
    return (
        grads * cosine
        + pltpu.roll(grads * sine_former, half_rot, 1)
        + pltpu.roll(grads * sine_latter, lanes - half_rot, 1)
    )


def whole(shape):
    return pl.BlockSpec(shape, lambda i, *_: (0,) * len(shape), pipeline_mode=pl.Buffered(1))


def kept_out(shape):
    return pl.BlockSpec(shape, lambda i, *_: (0,) * len(shape))


def allowed_keys(first_row, rows, keys, length):
    query = first_row + lax.broadcasted_iota(jnp.int32, (rows, keys), 0)
    key = lax.broadcasted_iota(jnp.int32, (rows, keys), 1)
    return (key <= query) & (key < length)


def attend_kernel(
    lengths_ref, wide_ref, weight_ref, maps_ref, bias_ref, cos_ref, sf_ref, sl_ref,
    q_ref, k_ref, v_ref, low_ref, att_ref, lse_ref, *, slot, steps
):
    rows = wide_ref.shape[0]
    own = q_ref.shape[1]
    width = weight_ref.shape[0]
    step = pl.program_id(0)
    length = lengths_ref[slot]
    heads = own // HEAD_DIM
    tables = (cos_ref[...], sf_ref[...], sl_ref[...])
    projected = (
        dot(wide_ref[:, :width], weight_ref[...])
        + bias_ref[...]
        + dot(wide_ref[:, width:], maps_ref[...])
    )
    head_lane = lax.broadcasted_iota(jnp.int32, (rows, own), 1) // HEAD_DIM
    lse_lane = lax.broadcasted_iota(jnp.int32, (rows, 128), 1)
    here = pl.ds(pl.multiple_of(step * rows, rows), rows)
    queries = (turn_rows(projected[:, :own], tables).astype(low)) * low(HEAD_DIM**-0.5)
    q_ref[here, :] = queries
    k_ref[here, :] = turn_rows(projected[:, own : 2 * own], tables).astype(low)
    v_ref[here, :] = projected[:, 2 * own :].astype(low)
    for i in range(steps):

        @pl.when(step == i)
        def _():
            span = (i + 1) * rows
            keys = k_ref[:span, :]
            values = v_ref[:span, :]
            allowed = allowed_keys(i * rows, rows, span, length)
            attended = jnp.zeros((rows, own), jnp.float32)
            lse = jnp.zeros((rows, 128), jnp.float32)
            for h in range(heads):
                scores = dot_nt(jnp.where(head_lane == h, queries, low(0)), keys)
                scores = jnp.where(allowed, scores, masked_score)
                top = jnp.max(scores, axis=1, keepdims=True)
                shifted = jnp.exp(scores - top)
                total = jnp.sum(shifted, axis=1, keepdims=True)
                probabilities = (shifted * (1.0 / total)).astype(low)
                attended = jnp.where(head_lane == h, dot(probabilities, values), attended)
                lse = jnp.where(lse_lane == h, top + jnp.log(total), lse)
            att_ref[...] = attended
            low_ref[...] = attended.astype(low)
            lse_ref[...] = lse


def attend(lengths, wide, weight, maps, bias, tables, slot):
    span, columns = wide.shape
    width, three_own = weight.shape
    own = three_own // 3
    rows = 256
    block = lambda n: pl.BlockSpec((rows, n), lambda i, *_: (i, 0))
    return pl.pallas_call(
        lambda *refs: attend_kernel(*refs, slot=slot, steps=span // rows),
        grid_spec=pltpu.PrefetchScalarGridSpec(
            num_scalar_prefetch=1,
            grid=(span // rows,),
            in_specs=[
                block(columns),
                whole(weight.shape),
                whole(maps.shape),
                whole(bias.shape),
                block(own),
                block(own),
                block(own),
            ],
            out_specs=[
                kept_out((span, own)),
                kept_out((span, own)),
                kept_out((span, own)),
                block(own),
                block(own),
                block(128),
            ],
        ),
        out_shape=[
            jax.ShapeDtypeStruct((span, own), low),
            jax.ShapeDtypeStruct((span, own), low),
            jax.ShapeDtypeStruct((span, own), low),
            jax.ShapeDtypeStruct((span, own), low),
            jax.ShapeDtypeStruct((span, own), jnp.float32),
            jax.ShapeDtypeStruct((span, 128), jnp.float32),
        ],
        compiler_params=pltpu.CompilerParams(vmem_limit_bytes=56 << 20),
        cost_estimate=pl.CostEstimate(
            flops=2 * span * columns * three_own + 16 * span * span * 64 * own // HEAD_DIM,
            bytes_accessed=2 * (span * columns + width * three_own),
            transcendentals=span * span,
        ),
        name="attend",
    )(lengths, wide, weight, maps, bias, *tables)


def attend_back_kernel(
    lengths_ref, q_ref, k_ref, v_ref, lse_ref, att_ref, g_ref, mid_ref, weight_ref, maps_ref,
    cos_ref, sf_ref, sl_ref, out_ref, b_ref, dq_ref, dk_ref, dv_ref, *, slot, steps
):
    rows = out_ref.shape[0]
    own = q_ref.shape[1]
    width = weight_ref.shape[0]
    heads = own // HEAD_DIM
    step = pl.program_id(0)
    length = lengths_ref[slot]
    head_lane = lax.broadcasted_iota(jnp.int32, (rows, own), 1) // HEAD_DIM

    @pl.when(step == 0)
    def _():
        dk_ref[...] = jnp.zeros_like(dk_ref)
        dv_ref[...] = jnp.zeros_like(dv_ref)
        b_ref[...] = jnp.zeros_like(b_ref)

    for i in range(steps):

        @pl.when(step == i)
        def _():
            span = (i + 1) * rows
            mine = slice(i * rows, (i + 1) * rows)
            queries, grads = (q_ref[mine, :], g_ref[mine, :])
            keys, values = (k_ref[:span, :], v_ref[:span, :])
            products = grads.astype(jnp.float32) * att_ref[mine, :]
            allowed = allowed_keys(i * rows, rows, span, length)
            dq = jnp.zeros((rows, own), jnp.float32)
            for h in range(heads):
                mask = head_lane == h
                query = jnp.where(mask, queries, low(0))
                grad = jnp.where(mask, grads, low(0))
                delta = jnp.sum(jnp.where(mask, products, 0.0), axis=1, keepdims=True)
                scores = dot_nt(query, keys)
                probabilities = jnp.where(
                    allowed, jnp.exp(scores - lse_ref[mine, h : h + 1]), 0.0
                )
                score_grad = (probabilities * (dot_nt(grad, values) - delta)).astype(low)
                dq = jnp.where(mask, dot(score_grad, keys), dq)
                dk_ref[:span, :] += dot_tn(score_grad, query)
                dv_ref[:span, :] += dot_tn(probabilities.astype(low), grad)
            dq_ref[mine, :] = dq * (HEAD_DIM**-0.5)

    @pl.when(step >= steps)
    def _():
        here = pl.ds(pl.multiple_of((step - steps) * rows, rows), rows)
        tables = (cos_ref[...], sf_ref[...], sl_ref[...])
        parts = (
            unturn_rows(dq_ref[here, :], tables).astype(low),
            unturn_rows(dk_ref[here, :], tables).astype(low),
            dv_ref[here, :].astype(low),
        )
        total = jnp.zeros((rows, width), jnp.float32)
        extra = jnp.zeros((rows, EXTRA), jnp.float32)
        for j, part in enumerate(parts):
            columns = slice(j * own, (j + 1) * own)
            total += dot_nt(part, weight_ref[:, columns])
            extra += dot_nt(part, maps_ref[:, columns])
            b_ref[:, columns] += adapter_scale * dot_tn(mid_ref[...], part)
        out_ref[:, :width] = total.astype(low)
        out_ref[:, width:] = extra.astype(low)


def attend_back(lengths, q, k, v, lse, att, grads, wide, weight, maps, tables, slot):
    span, own = q.shape
    width = weight.shape[0]
    rows = 256
    steps = span // rows
    late = lambda i: jnp.maximum(i - steps, 0)
    block = lambda n: pl.BlockSpec((rows, n), lambda i, *_: (late(i), 0))
    return pl.pallas_call(
        lambda *refs: attend_back_kernel(*refs, slot=slot, steps=steps),
        grid_spec=pltpu.PrefetchScalarGridSpec(
            num_scalar_prefetch=1,
            grid=(2 * steps,),
            in_specs=[
                whole(q.shape),
                whole(q.shape),
                whole(q.shape),
                whole(lse.shape),
                whole(att.shape),
                whole(grads.shape),
                pl.BlockSpec((rows, EXTRA), lambda i, *_: (late(i), width // EXTRA)),
                whole(weight.shape),
                whole(maps.shape),
                block(own),
                block(own),
                block(own),
            ],
            out_specs=[block(width + EXTRA), kept_out((EXTRA, 3 * own))],
            scratch_shapes=[pltpu.VMEM((span, own), jnp.float32)] * 3,
        ),
        out_shape=[
            jax.ShapeDtypeStruct((span, width + EXTRA), low),
            jax.ShapeDtypeStruct((EXTRA, 3 * own), jnp.float32),
        ],
        compiler_params=pltpu.CompilerParams(vmem_limit_bytes=56 << 20),
        cost_estimate=pl.CostEstimate(
            flops=2 * span * width * 3 * own + 40 * span * span * 64 * own // HEAD_DIM,
            bytes_accessed=2 * (span * width + width * 3 * own),
            transcendentals=span * span,
        ),
        name="attend_back",
    )(lengths, q, k, v, lse, att, grads, wide, weight, maps, *tables)


def mlp_kernel(
    wide_ref, grad_ref, gu_ref, down_ref, gate_map_ref, up_map_ref, down_map_ref,
    down_out_ref, two_out_ref, g_gate_ref, g_up_ref, g_down_ref
):
    width = down_ref.shape[1]

    @pl.when(pl.program_id(0) == 0)
    def _():
        g_gate_ref[...] = jnp.zeros_like(g_gate_ref)
        g_up_ref[...] = jnp.zeros_like(g_up_ref)
        g_down_ref[...] = jnp.zeros_like(g_down_ref)

    two, mids = (wide_ref[:, :width], wide_ref[:, width:])
    grad_mid = grad_ref[:, width:]
    gate = dot_nt(two, gu_ref[:, :width]) + dot_nt(mids, gate_map_ref[...])
    up = dot_nt(two, gu_ref[:, width:]) + dot_nt(mids, up_map_ref[...])
    hidden_grad = dot_nt(grad_ref[:, :width], down_ref[...]) + dot_nt(grad_mid, down_map_ref[...])
    sigmoid = 1.0 / (1.0 + jnp.exp(-gate))
    silu = gate * sigmoid
    activated = (silu * up).astype(low)
    gate_grad = (hidden_grad * up * sigmoid * (1.0 + gate * (1.0 - sigmoid))).astype(low)
    up_grad = (hidden_grad * silu).astype(low)
    two_out_ref[:, :width] = (
        dot(gate_grad, gu_ref[:, :width]) + dot(up_grad, gu_ref[:, width:])
    ).astype(low)
    two_out_ref[:, width:] = (
        dot(gate_grad, gate_map_ref[...]) + dot(up_grad, up_map_ref[...])
    ).astype(low)
    down_out_ref[:, :width] = dot(activated, down_ref[...]).astype(low)
    down_out_ref[:, width:] = dot(activated, down_map_ref[...]).astype(low)
    g_gate_ref[...] += dot_tn(mids, gate_grad)
    g_up_ref[...] += dot_tn(mids, up_grad)
    g_down_ref[...] += dot_tn(grad_mid, activated)


def mlp(wide, grad_wide, gate_up, down, gate_map, up_map, down_map):
    span, columns = wide.shape
    hidden = down.shape[0]
    rows = 256
    block = pl.BlockSpec((rows, columns), lambda i: (i, 0))
    grads = jax.ShapeDtypeStruct((EXTRA, hidden), jnp.float32)
    return pl.pallas_call(
        mlp_kernel,
        grid=(span // rows,),
        in_specs=[block, block]
        + [whole(x.shape) for x in (gate_up, down, gate_map, up_map, down_map)],
        out_specs=[block, block] + [kept_out((EXTRA, hidden))] * 3,
        out_shape=[jax.ShapeDtypeStruct((span, columns), low)] * 2 + [grads] * 3,
        compiler_params=pltpu.CompilerParams(vmem_limit_bytes=56 << 20),
        cost_estimate=pl.CostEstimate(
            flops=12 * span * columns * hidden,
            bytes_accessed=8 * span * columns + 6 * hidden * columns,
            transcendentals=span * hidden,
        ),
        name="mlp",
    )(wide, grad_wide, gate_up, down, gate_map, up_map, down_map)


def spread_columns(piece, first):
    return jnp.pad(piece, ((0, 0), (first, EXTRA - first - piece.shape[1])))


def pick_columns(table, adapter, blocks):
    width = ADAPTER_COUNT * RANK
    return jnp.concatenate(
        [
            lax.dynamic_slice_in_dim(table[:, j * width : (j + 1) * width], adapter * RANK, RANK, 1)
            for j in range(blocks)
        ],
        axis=1,
    )


def widen(*parts):
    rows = parts[0].shape[0]
    used = sum(part.shape[1] for part in parts[1:])
    return jnp.concatenate([*parts, jnp.zeros((rows, EXTRA - used), parts[0].dtype)], axis=1)


def gather_rows(rows):
    return lax.all_gather(rows, "shard", axis=0, tiled=True)


def scatter_rows(rows):
    return lax.psum_scatter(rows, "shard", scatter_dimension=0, tiled=True)


def per_device(
    tokens,
    lengths,
    slot_adapter_index,
    norm_gain_rows,
    norm_shift_rows,
    query_key_value_weight,
    query_key_value_bias,
    output_projection_weight,
    gate_up_projection,
    down_projection_weight,
    attention_adapter_input,
    attention_adapter_output,
    output_adapter_input,
    output_adapter_output,
    feedforward_adapter_input,
    feedforward_adapter_output,
    down_adapter_input,
    down_adapter_output,
    output_cotangent,
):
    slot_count, local_span, width = tokens.shape
    shards = lax.axis_size("shard")
    reps = lax.axis_size("rep")
    me = lax.axis_index("shard")
    span = local_span * shards
    own = width // shards
    hidden = gate_up_projection.shape[0]
    places = me * local_span + jnp.arange(local_span, dtype=jnp.int32)
    slots = range(slot_count)
    adapters = [slot_adapter_index[s] for s in slots]

    map_pieces = []
    for s in slots:
        a = adapters[s]
        rows_of = lambda table: lax.dynamic_slice_in_dim(table, a * RANK, RANK, 0).T
        map_pieces += [
            pick_columns(attention_adapter_input, a, 3),
            pick_columns(feedforward_adapter_input, a, 2),
            pick_columns(output_adapter_input, a, 1),
            rows_of(output_adapter_output),
            rows_of(down_adapter_output),
        ]
    maps = gather_rows(jnp.concatenate(map_pieces, axis=1)).reshape(width, slot_count, -1)

    weight_here = lax.all_to_all(
        query_key_value_weight.reshape(own, 3, shards, own), "shard", 2, 0, tiled=True
    ).reshape(width, 3 * own)
    bias_here = lax.dynamic_slice_in_dim(
        query_key_value_bias.reshape(3, width), me * own, own, 1
    ).reshape(1, 3 * own)
    output_full = gather_rows(output_projection_weight)
    tables = rotary_tables(span, own // HEAD_DIM)
    gate_up = gate_up_projection.reshape(hidden, 2 * width)

    kept = []
    for s in slots:
        a = adapters[s]
        own_maps = maps[:, s]
        qkv_in, mlp_in = (own_maps[:, :48], own_maps[:, 48:80])
        out_in, out_out, down_out = (own_maps[:, 80:96], own_maps[:, 96:112], own_maps[:, 112:128])
        valid = (places < lengths[s]).astype(jnp.float32)[:, None]
        inputs = tokens[s].astype(jnp.float32)
        grad_rows = output_cotangent[s].astype(jnp.float32) * valid
        grad_low = grad_rows.astype(low)
        down_mid_grad = (adapter_scale * dot(grad_low, down_out)).astype(low)
        normed, unit_one, inverse_one = layer_norm(inputs, norm_gain_rows[0], norm_shift_rows[0])
        normed = normed.astype(low)
        qkv_mid = dot(normed, qkv_in).astype(low)
        qkv_out = lax.dynamic_slice_in_dim(attention_adapter_output, a * RANK, RANK, 1) * low(2)
        mlp_out = lax.dynamic_slice_in_dim(feedforward_adapter_output, a * RANK, RANK, 2) * low(2)
        kept.append(
            dict(
                qkv_in=qkv_in,
                mlp_in=mlp_in,
                out_in=out_in,
                out_out=out_out,
                down_out=down_out,
                valid=valid,
                inputs=inputs,
                grad_rows=grad_rows,
                grad_low=grad_low,
                down_mid_grad=down_mid_grad,
                normed=normed,
                unit_one=unit_one,
                inverse_one=inverse_one,
                qkv_mid=qkv_mid,
                qkv_map=jnp.concatenate(
                    [
                        jnp.pad(qkv_out[j], ((j * RANK, EXTRA - (j + 1) * RANK), (0, 0)))
                        for j in range(3)
                    ],
                    axis=1,
                ),
                gate_map=spread_columns(mlp_out[:, 0], 0),
                up_map=spread_columns(mlp_out[:, 1], RANK),
                down_map=spread_columns(
                    lax.dynamic_slice_in_dim(down_adapter_input, a * RANK, RANK, 1), 0
                ),
            )
        )

    for s in slots:
        k = kept[s]
        k["wide"] = gather_rows(widen(k["normed"], k["qkv_mid"]))
        k["q"], k["k"], k["v"], k["attended_low"], k["attended"], k["lse"] = attend(
            lengths, k["wide"], weight_here, k["qkv_map"], bias_here, tables, s
        )

    for s in slots:
        k = kept[s]
        attended = lax.all_to_all(k["attended_low"], "shard", 0, 1, tiled=True)
        out_mid = dot(attended, k["out_in"]).astype(low)
        hidden_in = k["inputs"] + (
            dot(attended, output_full) + adapter_scale * dot_nt(out_mid, k["out_out"])
        )
        normed_two, unit_two, inverse_two = layer_norm(
            hidden_in, norm_gain_rows[1], norm_shift_rows[1]
        )
        normed_two = normed_two.astype(low)
        mlp_mid = dot(normed_two, k["mlp_in"]).astype(low)
        k.update(
            attended_rows=attended,
            out_mid=out_mid,
            hidden_in=hidden_in,
            normed_two=normed_two,
            unit_two=unit_two,
            inverse_two=inverse_two,
            mlp_mid=mlp_mid,
        )

    for s in slots:
        k = kept[s]
        wide = gather_rows(widen(k["normed_two"], k["mlp_mid"]))
        grad_wide = gather_rows(widen(k["grad_low"], k["down_mid_grad"]))
        down_partial, two_partial, k["g_gate"], k["g_up"], k["g_down"] = mlp(
            wide,
            grad_wide,
            gate_up,
            down_projection_weight,
            k["gate_map"],
            k["up_map"],
            k["down_map"],
        )
        k["two_sum"] = scatter_rows(two_partial)
        k["down_sum"] = scatter_rows(down_partial)

    for s in slots:
        k = kept[s]
        mlp_mid_grad = k["two_sum"][:, width : width + 2 * RANK]
        two_grad = k["two_sum"][:, :width].astype(jnp.float32) + dot_nt(mlp_mid_grad, k["mlp_in"])
        residual_grad = k["grad_rows"] + layer_norm_back(
            two_grad, k["unit_two"], k["inverse_two"], norm_gain_rows[1]
        )
        branch = residual_grad.astype(low)
        out_mid_grad = (adapter_scale * dot(branch, k["out_out"])).astype(low)
        attended_grad = (dot_nt(branch, output_full) + dot_nt(out_mid_grad, k["out_in"])).astype(
            low
        )
        k.update(
            residual_grad=residual_grad,
            branch=branch,
            mlp_mid_grad=mlp_mid_grad,
            out_mid_grad=out_mid_grad,
        )
        k["head_grad"] = lax.all_to_all(attended_grad, "shard", 1, 0, tiled=True)

    for s in slots:
        k = kept[s]
        one_partial, k["qkv_b"] = attend_back(
            lengths,
            k["q"],
            k["k"],
            k["v"],
            k["lse"],
            k["attended"],
            k["head_grad"],
            k["wide"],
            weight_here,
            k["qkv_map"],
            tables,
            s,
        )
        k["one_sum"] = scatter_rows(one_partial)

    block_parts = []
    token_parts = []
    compact = []
    for s in slots:
        k = kept[s]
        down_mid = k["down_sum"][:, width : width + RANK]
        feed = k["down_sum"][:, :width].astype(jnp.float32) + adapter_scale * dot_nt(
            down_mid, k["down_out"]
        )
        block_parts.append(((k["hidden_in"] + feed) * k["valid"]).astype(low))
        mid_grad = k["one_sum"][:, width : width + 3 * RANK]
        normed_grad = k["one_sum"][:, :width].astype(jnp.float32) + dot_nt(mid_grad, k["qkv_in"])
        token_parts.append(
            k["residual_grad"]
            + layer_norm_back(normed_grad, k["unit_one"], k["inverse_one"], norm_gain_rows[0])
        )
        compact += [
            dot_tn(mid_grad, k["normed"]),
            dot_tn(k["mlp_mid_grad"], k["normed_two"]),
            dot_tn(k["out_mid_grad"], k["attended_rows"]),
            adapter_scale * dot_tn(k["out_mid"], k["branch"]),
            adapter_scale * dot_tn(down_mid, k["grad_low"]),
        ]
    compact = jnp.concatenate(compact, axis=0).astype(low)
    columns = compact.shape[0]
    owned = scatter_rows(
        compact.reshape(columns, shards, own).transpose(1, 0, 2).reshape(shards * columns, own)
    ).reshape(slot_count, 8, RANK, own)

    grads = []
    for s in slots:
        k = kept[s]
        part = [owned[s, j] for j in range(8)]
        part += [
            k["qkv_b"][j * RANK : (j + 1) * RANK, j * own : (j + 1) * own].astype(low)
            for j in range(3)
        ]
        part += [
            (adapter_scale * k["g_gate"][:RANK]).astype(low),
            (adapter_scale * k["g_up"][RANK : 2 * RANK]).astype(low),
            k["g_down"][:RANK].astype(low),
        ]
        grads.append(jnp.concatenate(part, axis=1))
    shared = lax.all_gather(jnp.stack(grads), "rep", axis=0, tiled=True)
    index = lax.all_gather(slot_adapter_index, "rep", axis=0, tiled=True)
    spread = (index[:, None] == jnp.arange(ADAPTER_COUNT, dtype=jnp.int32)[None, :]).astype(
        jnp.float32
    )
    full = jnp.sum(
        shared.astype(jnp.float32)[:, None] * spread[:, :, None, None], axis=0
    ).reshape(ADAPTER_COUNT * RANK, shared.shape[2])
    pieces = [full[:, j * own : (j + 1) * own] for j in range(11)]
    rest = [full[:, 11 * own + j * hidden : 11 * own + (j + 1) * hidden] for j in range(3)]
    return (
        jnp.stack(block_parts),
        jnp.stack(token_parts),
        jnp.concatenate([piece.T for piece in pieces[:3]], axis=1),
        jnp.stack(pieces[8:11]),
        pieces[5].T,
        pieces[6],
        jnp.concatenate([piece.T for piece in pieces[3:5]], axis=1),
        jnp.stack([rest[0].T, rest[1].T], axis=1),
        rest[2].T,
        pieces[7],
    )


def solution(mesh):
    rows = P("shard", None)
    in_specs = (
        P("rep", "shard", None),
        P("rep"),
        P("rep"),
        P(),
        P(),
        rows,
        P(),
        rows,
        P("shard", None, None),
        rows,
        rows,
        P(None, None, "shard"),
        rows,
        P(None, "shard"),
        rows,
        P("shard", None, None),
        rows,
        P(None, "shard"),
        P("rep", "shard", None),
    )
    out_specs = (
        P("rep", "shard", None),
        P("rep", "shard", None),
        rows,
        P(None, None, "shard"),
        rows,
        P(None, "shard"),
        rows,
        P("shard", None, None),
        rows,
        P(None, "shard"),
    )
    return jax.shard_map(
        per_device, mesh=mesh, in_specs=in_specs, out_specs=out_specs, check_vma=False
    )
```

```python
import math

import jax
import jax.numpy as jnp
from jax import lax
from jax.experimental import pallas as pl
from jax.experimental.pallas import tpu as pltpu
from jax.sharding import PartitionSpec as P

HEAD_DIM = 64
ROT = 16
ADAPTER_COUNT = 8
RANK = 16
EXTRA = 128

adapter_scale = 2.0
norm_epsilon = 1e-05
rotary_base = 10000.0
masked_score = -1e30
low = jnp.bfloat16


def dot(a, b):
    return jnp.dot(a, b, preferred_element_type=jnp.float32)


def dot_nt(a, b):
    return lax.dot_general(a, b, (((1,), (1,)), ((), ())), preferred_element_type=jnp.float32)


def dot_tn(a, b):
    return lax.dot_general(a, b, (((0,), (0,)), ((), ())), preferred_element_type=jnp.float32)


def layer_norm(values, gain_row, shift_row):
    average = jnp.mean(values, axis=-1, keepdims=True)
    centered = values - average
    variance = jnp.mean(centered * centered, axis=-1, keepdims=True)
    inverse = lax.rsqrt(variance + norm_epsilon)
    unit_rows = centered * inverse
    return (unit_rows * gain_row + shift_row, unit_rows, inverse)


def layer_norm_back(grad_rows, unit_rows, inverse, gain_row):
    scaled = grad_rows * gain_row
    return inverse * (
        scaled
        - jnp.mean(scaled, axis=-1, keepdims=True)
        - unit_rows * jnp.mean(scaled * unit_rows, axis=-1, keepdims=True)
    )


def rotary_tables(span, heads_here):
    half_rot = ROT // 2
    lane = jnp.arange(heads_here * HEAD_DIM, dtype=jnp.int32) % HEAD_DIM
    turn = (lane % half_rot).astype(jnp.float32) * (-2.0 * math.log(rotary_base) / ROT)
    places = jnp.arange(span, dtype=jnp.int32).astype(jnp.float32)
    angles = places[:, None] * jnp.exp(turn)[None, :]
    cosine = jnp.where(lane[None, :] < ROT, jnp.cos(angles), 1.0)
    sine = jnp.sin(angles)
    sine_former = jnp.where(lane[None, :] < half_rot, -sine, 0.0)
    sine_latter = jnp.where((lane[None, :] >= half_rot) & (lane[None, :] < ROT), sine, 0.0)
    return (cosine, sine_former, sine_latter)


def turn_rows(values, tables):
    cosine, sine_former, sine_latter = tables
    half_rot = ROT // 2
    lanes = values.shape[1]
    return (
        values * cosine
        + pltpu.roll(values, lanes - half_rot, 1) * sine_former
        + pltpu.roll(values, half_rot, 1) * sine_latter
    )


def unturn_rows(grads, tables):
    cosine, sine_former, sine_latter = tables
    half_rot = ROT // 2
    lanes = grads.shape[1]
    return (
        grads * cosine
        + pltpu.roll(grads * sine_former, half_rot, 1)
        + pltpu.roll(grads * sine_latter, lanes - half_rot, 1)
    )


def whole(shape):
    return pl.BlockSpec(shape, lambda i, *_: (0,) * len(shape), pipeline_mode=pl.Buffered(1))


def kept_out(shape):
    return pl.BlockSpec(shape, lambda i, *_: (0,) * len(shape))


def allowed_keys(first_row, rows, keys, length):
    query = first_row + lax.broadcasted_iota(jnp.int32, (rows, keys), 0)
    key = lax.broadcasted_iota(jnp.int32, (rows, keys), 1)
    return (key <= query) & (key < length)


def chip_rows(order_ref, oa_ref, ob_ref, pa_ref, pb_ref):
    mine = jnp.concatenate([oa_ref[0], ob_ref[0]], axis=0)
    other = jnp.concatenate([pa_ref[0], pb_ref[0]], axis=0)
    first = order_ref[0] == 0
    return jnp.concatenate(
        [jnp.where(first, mine, other), jnp.where(first, other, mine)], axis=0
    )


def piece_specs(pieces):
    chips, rows, columns = pieces[0].shape
    half_a = pl.BlockSpec((1, rows, columns), lambda i, _, o: (o[1 + i], 0, 0))
    half_b = pl.BlockSpec((1, rows, columns), lambda i, _, o: (o[1 + chips + i], 0, 0))
    return [half_a, half_b, half_a, half_b]


def split_cores(order_ref, rows, keep_ref, give_ref, columns):
    half = rows.shape[0] // 2
    first = order_ref[0] == 0
    keep_ref[0, :, columns] = jnp.where(first, rows[:half], rows[half:])
    give_ref[0, :, columns] = jnp.where(first, rows[half:], rows[:half])


def attend_kernel(
    lengths_ref, order_ref, oa_ref, ob_ref, pa_ref, pb_ref, weight_ref, in_ref, maps_ref, bias_ref,
    cos_ref, sf_ref, sl_ref, q_ref, k_ref, v_ref, low_ref, att_ref, lse_ref, mid_ref, *, slot, steps
):
    rows = cos_ref.shape[0]
    own = q_ref.shape[1]
    normed = chip_rows(order_ref, oa_ref, ob_ref, pa_ref, pb_ref)
    step = pl.program_id(0)
    length = lengths_ref[slot]
    heads = own // HEAD_DIM
    tables = (cos_ref[...], sf_ref[...], sl_ref[...])
    mids = dot(normed, in_ref[...]).astype(low)
    mid_ref[...] = mids
    projected = dot(normed, weight_ref[...]) + bias_ref[...] + dot(mids, maps_ref[...])
    head_lane = lax.broadcasted_iota(jnp.int32, (rows, own), 1) // HEAD_DIM
    lse_lane = lax.broadcasted_iota(jnp.int32, (rows, 128), 1)
    here = pl.ds(pl.multiple_of(step * rows, rows), rows)
    queries = (turn_rows(projected[:, :own], tables).astype(low)) * low(HEAD_DIM**-0.5)
    q_ref[here, :] = queries
    k_ref[here, :] = turn_rows(projected[:, own : 2 * own], tables).astype(low)
    v_ref[here, :] = projected[:, 2 * own :].astype(low)
    for i in range(steps):

        @pl.when(step == i)
        def _():
            span = (i + 1) * rows
            keys = k_ref[:span, :]
            values = v_ref[:span, :]
            allowed = allowed_keys(i * rows, rows, span, length)
            attended = jnp.zeros((rows, own), jnp.float32)
            lse = jnp.zeros((rows, 128), jnp.float32)
            for h in range(heads):
                scores = dot_nt(jnp.where(head_lane == h, queries, low(0)), keys)
                scores = jnp.where(allowed, scores, masked_score)
                top = jnp.max(scores, axis=1, keepdims=True)
                shifted = jnp.exp(scores - top)
                total = jnp.sum(shifted, axis=1, keepdims=True)
                probabilities = (shifted * (1.0 / total)).astype(low)
                attended = jnp.where(head_lane == h, dot(probabilities, values), attended)
                lse = jnp.where(lse_lane == h, top + jnp.log(total), lse)
            att_ref[...] = attended
            low_ref[...] = attended.astype(low)
            lse_ref[...] = lse


def attend(lengths, order, pieces, weight, map_in, maps, bias, tables, slot):
    width, three_own = weight.shape
    own = three_own // 3
    rows = 2 * 2 * pieces[0].shape[1]
    span = rows * pieces[0].shape[0]
    block = lambda n: pl.BlockSpec((rows, n), lambda i, *_: (i, 0))
    return pl.pallas_call(
        lambda *refs: attend_kernel(*refs, slot=slot, steps=span // rows),
        grid_spec=pltpu.PrefetchScalarGridSpec(
            num_scalar_prefetch=2,
            grid=(span // rows,),
            in_specs=piece_specs(pieces)
            + [whole(x.shape) for x in (weight, map_in, maps, bias)]
            + [block(own)] * 3,
            out_specs=[
                kept_out((span, own)),
                kept_out((span, own)),
                kept_out((span, own)),
                block(own),
                block(own),
                block(128),
                block(EXTRA),
            ],
        ),
        out_shape=[jax.ShapeDtypeStruct((span, own), low)] * 4
        + [
            jax.ShapeDtypeStruct((span, own), jnp.float32),
            jax.ShapeDtypeStruct((span, 128), jnp.float32),
            jax.ShapeDtypeStruct((span, EXTRA), low),
        ],
        compiler_params=pltpu.CompilerParams(vmem_limit_bytes=56 << 20),
        cost_estimate=pl.CostEstimate(
            flops=2 * span * width * three_own + 16 * span * span * own,
            bytes_accessed=2 * (span * width + width * three_own),
            transcendentals=span * span,
        ),
        name="attend",
    )(lengths, order, *pieces, weight, map_in, maps, bias, *tables)


def attend_back_kernel(
    lengths_ref, order_ref, q_ref, k_ref, v_ref, lse_ref, att_ref, g_ref, mid_ref, weight_ref,
    maps_ref, cos_ref, sf_ref, sl_ref, keep_ref, give_ref, b_ref, dq_ref, dk_ref, dv_ref,
    *, slot, steps
):
    rows = cos_ref.shape[0]
    own = q_ref.shape[1]
    width = weight_ref.shape[0]
    heads = own // HEAD_DIM
    step = pl.program_id(0)
    length = lengths_ref[slot]
    head_lane = lax.broadcasted_iota(jnp.int32, (rows, own), 1) // HEAD_DIM

    @pl.when(step == 0)
    def _():
        dk_ref[...] = jnp.zeros_like(dk_ref)
        dv_ref[...] = jnp.zeros_like(dv_ref)
        b_ref[...] = jnp.zeros_like(b_ref)

    for i in range(steps):

        @pl.when(step == i)
        def _():
            span = (i + 1) * rows
            mine = slice(i * rows, (i + 1) * rows)
            queries, grads = (q_ref[mine, :], g_ref[mine, :])
            keys, values = (k_ref[:span, :], v_ref[:span, :])
            products = grads.astype(jnp.float32) * att_ref[mine, :]
            allowed = allowed_keys(i * rows, rows, span, length)
            dq = jnp.zeros((rows, own), jnp.float32)
            for h in range(heads):
                mask = head_lane == h
                query = jnp.where(mask, queries, low(0))
                grad = jnp.where(mask, grads, low(0))
                delta = jnp.sum(jnp.where(mask, products, 0.0), axis=1, keepdims=True)
                scores = dot_nt(query, keys)
                probabilities = jnp.where(
                    allowed, jnp.exp(scores - lse_ref[mine, h : h + 1]), 0.0
                )
                score_grad = (probabilities * (dot_nt(grad, values) - delta)).astype(low)
                dq = jnp.where(mask, dot(score_grad, keys), dq)
                dk_ref[:span, :] += dot_tn(score_grad, query)
                dv_ref[:span, :] += dot_tn(probabilities.astype(low), grad)
            dq_ref[mine, :] = dq * (HEAD_DIM**-0.5)

    @pl.when(step >= steps)
    def _():
        here = pl.ds(pl.multiple_of((step - steps) * rows, rows), rows)
        tables = (cos_ref[...], sf_ref[...], sl_ref[...])
        parts = (
            unturn_rows(dq_ref[here, :], tables).astype(low),
            unturn_rows(dk_ref[here, :], tables).astype(low),
            dv_ref[here, :].astype(low),
        )
        total = jnp.zeros((rows, width), jnp.float32)
        extra = jnp.zeros((rows, EXTRA), jnp.float32)
        for j, part in enumerate(parts):
            columns = slice(j * own, (j + 1) * own)
            total += dot_nt(part, weight_ref[:, columns])
            extra += dot_nt(part, maps_ref[:, columns])
            b_ref[:, columns] += adapter_scale * dot_tn(mid_ref[...], part)
        split_cores(order_ref, total.astype(low), keep_ref, give_ref, slice(0, width))
        split_cores(order_ref, extra.astype(low), keep_ref, give_ref, slice(width, width + EXTRA))


def attend_back(lengths, order, chips, q, k, v, lse, att, grads, mids, weight, maps, tables, slot):
    span, own = q.shape
    width = weight.shape[0]
    steps = chips
    rows = span // steps
    late = lambda i: jnp.maximum(i - steps, 0)
    block = lambda n: pl.BlockSpec((rows, n), lambda i, *_: (late(i), 0))
    return pl.pallas_call(
        lambda *refs: attend_back_kernel(*refs, slot=slot, steps=steps),
        grid_spec=pltpu.PrefetchScalarGridSpec(
            num_scalar_prefetch=2,
            grid=(2 * steps,),
            in_specs=[
                whole(q.shape),
                whole(q.shape),
                whole(q.shape),
                whole(lse.shape),
                whole(att.shape),
                whole(grads.shape),
                block(EXTRA),
                whole(weight.shape),
                whole(maps.shape),
                block(own),
                block(own),
                block(own),
            ],
            out_specs=[
                pl.BlockSpec(
                    (1, rows // 2, width + EXTRA),
                    lambda i, _, o: (o[1 + 2 * steps + late(i)], 0, 0),
                )
            ]
            * 2
            + [kept_out((EXTRA, 3 * own))],
            scratch_shapes=[pltpu.VMEM((span, own), jnp.float32)] * 3,
        ),
        out_shape=[jax.ShapeDtypeStruct((chips, rows // 2, width + EXTRA), low)] * 2
        + [jax.ShapeDtypeStruct((EXTRA, 3 * own), jnp.float32)],
        compiler_params=pltpu.CompilerParams(vmem_limit_bytes=56 << 20),
        cost_estimate=pl.CostEstimate(
            flops=2 * span * width * 3 * own + 40 * span * span * own,
            bytes_accessed=2 * (span * width + width * 3 * own),
            transcendentals=span * span,
        ),
        name="attend_back",
    )(lengths, order, q, k, v, lse, att, grads, mids, weight, maps, *tables)


def mlp_kernel(
    lengths_ref, order_ref, oa_ref, ob_ref, pa_ref, pb_ref, grad_ref, gu_ref, down_ref, in_ref,
    out_map_ref, gate_map_ref, up_map_ref, down_map_ref,
    down_out_ref, keep_ref, give_ref, g_gate_ref, g_up_ref, g_down_ref
):
    width = down_ref.shape[1]

    @pl.when(pl.program_id(0) == 0)
    def _():
        g_gate_ref[...] = jnp.zeros_like(g_gate_ref)
        g_up_ref[...] = jnp.zeros_like(g_up_ref)
        g_down_ref[...] = jnp.zeros_like(g_down_ref)

    two = chip_rows(order_ref, oa_ref, ob_ref, pa_ref, pb_ref)
    grads = jnp.concatenate([grad_ref[0, 0], grad_ref[1, 0]], axis=0)
    mids = dot(two, in_ref[...]).astype(low)
    grad_mid = (adapter_scale * dot(grads, out_map_ref[...])).astype(low)
    gate = dot_nt(two, gu_ref[:, :width]) + dot_nt(mids, gate_map_ref[...])
    up = dot_nt(two, gu_ref[:, width:]) + dot_nt(mids, up_map_ref[...])
    hidden_grad = dot_nt(grads, down_ref[...]) + dot_nt(grad_mid, down_map_ref[...])
    sigmoid = 1.0 / (1.0 + jnp.exp(-gate))
    silu = gate * sigmoid
    activated = (silu * up).astype(low)
    gate_grad = (hidden_grad * up * sigmoid * (1.0 + gate * (1.0 - sigmoid))).astype(low)
    up_grad = (hidden_grad * silu).astype(low)
    total = dot(gate_grad, gu_ref[:, :width]) + dot(up_grad, gu_ref[:, width:])
    extra = dot(gate_grad, gate_map_ref[...]) + dot(up_grad, up_map_ref[...])
    split_cores(order_ref, total.astype(low), keep_ref, give_ref, slice(0, width))
    split_cores(order_ref, extra.astype(low), keep_ref, give_ref, slice(width, width + EXTRA))
    down_out_ref[:, :width] = dot(activated, down_ref[...]).astype(low)
    down_out_ref[:, width:] = dot(activated, down_map_ref[...]).astype(low)
    g_gate_ref[...] += dot_tn(mids, gate_grad)
    g_up_ref[...] += dot_tn(mids, up_grad)
    g_down_ref[...] += dot_tn(grad_mid, activated)


def mlp(lengths, order, pieces, grads, slot, gate_up, down, map_in, out_map, gate_map, up_map, down_map):
    chips = pieces[0].shape[0]
    local_span, width = grads.shape[2:]
    hidden = down.shape[0]
    rows = 2 * local_span
    span = chips * rows
    columns = width + EXTRA
    sums = jax.ShapeDtypeStruct((EXTRA, hidden), jnp.float32)
    halves = pl.BlockSpec((1, rows // 2, columns), lambda i, _, o: (o[1 + 2 * chips + i], 0, 0))
    weights = (gate_up, down, map_in, out_map, gate_map, up_map, down_map)
    return pl.pallas_call(
        mlp_kernel,
        grid_spec=pltpu.PrefetchScalarGridSpec(
            num_scalar_prefetch=2,
            grid=(chips,),
            in_specs=piece_specs(pieces)
            + [pl.BlockSpec((2, 1, local_span, width), lambda i, *_: (i, slot, 0, 0))]
            + [whole(x.shape) for x in weights],
            out_specs=[pl.BlockSpec((rows, columns), lambda i, *_: (i, 0)), halves, halves]
            + [kept_out((EXTRA, hidden))] * 3,
        ),
        out_shape=[jax.ShapeDtypeStruct((span, columns), low)]
        + [jax.ShapeDtypeStruct((chips, rows // 2, columns), low)] * 2
        + [sums] * 3,
        compiler_params=pltpu.CompilerParams(vmem_limit_bytes=56 << 20),
        cost_estimate=pl.CostEstimate(
            flops=12 * span * columns * hidden,
            bytes_accessed=8 * span * columns + 6 * hidden * columns,
            transcendentals=span * hidden,
        ),
        name="mlp",
    )(lengths, order, *pieces, grads, *weights)


def spread_columns(piece, first):
    return jnp.pad(piece, ((0, 0), (first, EXTRA - first - piece.shape[1])))


def pick_columns(table, adapter, blocks):
    width = ADAPTER_COUNT * RANK
    return jnp.concatenate(
        [
            lax.dynamic_slice_in_dim(table[:, j * width : (j + 1) * width], adapter * RANK, RANK, 1)
            for j in range(blocks)
        ],
        axis=1,
    )


def hop(array, bit):
    count = lax.axis_size("shard")
    return lax.ppermute(array, "shard", [(i, i ^ bit) for i in range(count)])


def chip_bits():
    return [bit for bit in (2, 4, 8, 16) if bit < lax.axis_size("shard")]


def gather_hops(rows):
    half = rows.shape[0] // 2
    bits = chip_bits()
    held = []
    for part, order in ((rows[:half], bits), (rows[half:], bits[::-1])):
        stack = part[None]
        for bit in order:
            stack = jnp.concatenate([stack, hop(stack, bit)], axis=0)
        held.append(stack)
    return (held[0], held[1], hop(held[0], 1), hop(held[1], 1))


def piece_order(me):
    bits = chip_bits()
    chips = 2 ** len(bits)
    relative = jnp.arange(chips, dtype=jnp.int32) ^ (me // 2)

    def place(order):
        return sum((((relative * 2) // bit) % 2) << step for step, bit in enumerate(order))

    return jnp.concatenate([(me % 2)[None], place(bits), place(bits[::-1]), relative]).astype(
        jnp.int32
    )


def add_low(a, b):
    return a.astype(jnp.float32) + b.astype(jnp.float32)


def scatter_hops(keep, give):
    half = keep.shape[1] // 2
    bits = chip_bits()
    got = hop(give, 1)
    sums = []
    for rows, order in ((slice(0, half), bits), (slice(half, 2 * half), bits[::-1])):
        blocks = {r: add_low(keep[r, rows], got[r, rows]) for r in range(keep.shape[0])}
        for bit in order:
            away = [r for r in blocks if (r * 2) & bit]
            sent = hop(jnp.stack([blocks[r] for r in away]).astype(low), bit)
            blocks = {
                r ^ (bit // 2): blocks[r ^ (bit // 2)] + sent[n].astype(jnp.float32)
                for n, r in enumerate(away)
            }
        sums.append(blocks[0])
    return jnp.concatenate(sums, axis=0)


def scatter_small(blocks):
    count = blocks.shape[0]
    me = lax.axis_index("shard")
    blocks = blocks.astype(low)
    bit = count // 2
    held = blocks
    while bit:
        split = held.reshape(2, bit, *held.shape[1:])
        mine = (me // bit) % 2
        keep = jnp.where(mine == 0, split[0], split[1])
        give = jnp.where(mine == 0, split[1], split[0])
        held = add_low(keep, hop(give, bit)).astype(low if bit > 1 else jnp.float32)
        bit //= 2
    return held[0]


def gather_rows(rows):
    return lax.all_gather(rows, "shard", axis=0, tiled=True)


def scatter_rows(rows):
    return lax.psum_scatter(rows, "shard", scatter_dimension=0, tiled=True)


def per_device(
    tokens,
    lengths,
    slot_adapter_index,
    norm_gain_rows,
    norm_shift_rows,
    query_key_value_weight,
    query_key_value_bias,
    output_projection_weight,
    gate_up_projection,
    down_projection_weight,
    attention_adapter_input,
    attention_adapter_output,
    output_adapter_input,
    output_adapter_output,
    feedforward_adapter_input,
    feedforward_adapter_output,
    down_adapter_input,
    down_adapter_output,
    output_cotangent,
):
    slot_count, local_span, width = tokens.shape
    shards = lax.axis_size("shard")
    me = lax.axis_index("shard")
    span = local_span * shards
    own = width // shards
    hidden = gate_up_projection.shape[0]
    places = me * local_span + jnp.arange(local_span, dtype=jnp.int32)
    slots = range(slot_count)
    adapters = [slot_adapter_index[s] for s in slots]

    map_pieces = []
    for s in slots:
        a = adapters[s]
        rows_of = lambda table: lax.dynamic_slice_in_dim(table, a * RANK, RANK, 0).T
        map_pieces += [
            pick_columns(attention_adapter_input, a, 3),
            pick_columns(feedforward_adapter_input, a, 2),
            pick_columns(output_adapter_input, a, 1),
            rows_of(output_adapter_output),
            rows_of(down_adapter_output),
        ]
    maps = gather_rows(jnp.concatenate(map_pieces, axis=1)).reshape(width, slot_count, -1)

    weight_here = lax.all_to_all(
        query_key_value_weight.reshape(own, 3, shards, own)
        .transpose(2, 0, 1, 3)
        .reshape(shards, own, 3 * own),
        "shard",
        0,
        0,
        tiled=True,
    ).reshape(width, 3 * own)
    bias_here = lax.dynamic_slice_in_dim(
        query_key_value_bias.reshape(3, width), me * own, own, 1
    ).reshape(1, 3 * own)
    output_full = gather_rows(output_projection_weight)
    tables = rotary_tables(span, own // HEAD_DIM)
    order = piece_order(me)
    chips = shards // 2
    valid_all = (places[None, :] < lengths[:, None]).astype(jnp.float32)[:, :, None]
    grad_all = output_cotangent.astype(jnp.float32) * valid_all
    grad_low_all = grad_all.astype(low)
    grad_wide = gather_rows(grad_low_all.reshape(slot_count * local_span, width)).reshape(
        shards, slot_count, local_span, width
    )
    gate_up = gate_up_projection.reshape(hidden, 2 * width)

    kept = []
    for s in slots:
        a = adapters[s]
        own_maps = maps[:, s]
        qkv_in, mlp_in = (own_maps[:, :48], own_maps[:, 48:80])
        out_in, out_out, down_out = (own_maps[:, 80:96], own_maps[:, 96:112], own_maps[:, 112:128])
        valid = valid_all[s]
        inputs = tokens[s].astype(jnp.float32)
        grad_rows = grad_all[s]
        grad_low = grad_low_all[s]
        normed, unit_one, inverse_one = layer_norm(inputs, norm_gain_rows[0], norm_shift_rows[0])
        normed = normed.astype(low)
        qkv_out = lax.dynamic_slice_in_dim(attention_adapter_output, a * RANK, RANK, 1) * low(2)
        mlp_out = lax.dynamic_slice_in_dim(feedforward_adapter_output, a * RANK, RANK, 2) * low(2)
        kept.append(
            dict(
                qkv_in=qkv_in,
                mlp_in=mlp_in,
                out_in=out_in,
                out_out=out_out,
                down_out=down_out,
                valid=valid,
                inputs=inputs,
                grad_rows=grad_rows,
                grad_low=grad_low,
                normed=normed,
                unit_one=unit_one,
                inverse_one=inverse_one,
                qkv_map=jnp.concatenate(
                    [
                        jnp.pad(qkv_out[j], ((j * RANK, EXTRA - (j + 1) * RANK), (0, 0)))
                        for j in range(3)
                    ],
                    axis=1,
                ),
                gate_map=spread_columns(mlp_out[:, 0], 0),
                up_map=spread_columns(mlp_out[:, 1], RANK),
                down_map=spread_columns(
                    lax.dynamic_slice_in_dim(down_adapter_input, a * RANK, RANK, 1), 0
                ),
            )
        )

    for s in slots:
        k = kept[s]
        pieces = gather_hops(k["normed"])
        k["q"], k["k"], k["v"], k["attended_low"], k["attended"], k["lse"], k["mids"] = attend(
            lengths,
            order,
            pieces,
            weight_here,
            spread_columns(k["qkv_in"], 0),
            k["qkv_map"],
            bias_here,
            tables,
            s,
        )

    for s in slots:
        k = kept[s]
        attended = lax.all_to_all(k["attended_low"], "shard", 0, 1, tiled=True)
        out_mid = dot(attended, k["out_in"]).astype(low)
        hidden_in = k["inputs"] + (
            dot(attended, output_full) + adapter_scale * dot_nt(out_mid, k["out_out"])
        )
        normed_two, unit_two, inverse_two = layer_norm(
            hidden_in, norm_gain_rows[1], norm_shift_rows[1]
        )
        normed_two = normed_two.astype(low)
        k.update(
            attended_rows=attended,
            out_mid=out_mid,
            hidden_in=hidden_in,
            normed_two=normed_two,
            unit_two=unit_two,
            inverse_two=inverse_two,
        )

    for s in slots:
        k = kept[s]
        down_partial, keep, give, k["g_gate"], k["g_up"], k["g_down"] = mlp(
            lengths,
            order,
            gather_hops(k["normed_two"]),
            grad_wide,
            s,
            gate_up,
            down_projection_weight,
            spread_columns(k["mlp_in"], 0),
            spread_columns(k["down_out"], 0),
            k["gate_map"],
            k["up_map"],
            k["down_map"],
        )
        k["two_sum"] = scatter_hops(keep, give)
        k["down_sum"] = scatter_rows(down_partial)

    for s in slots:
        k = kept[s]
        mlp_mid_grad = k["two_sum"][:, width : width + 2 * RANK].astype(low)
        two_grad = k["two_sum"][:, :width] + dot_nt(mlp_mid_grad, k["mlp_in"])
        residual_grad = k["grad_rows"] + layer_norm_back(
            two_grad, k["unit_two"], k["inverse_two"], norm_gain_rows[1]
        )
        branch = residual_grad.astype(low)
        out_mid_grad = (adapter_scale * dot(branch, k["out_out"])).astype(low)
        attended_grad = (dot_nt(branch, output_full) + dot_nt(out_mid_grad, k["out_in"])).astype(
            low
        )
        k.update(
            residual_grad=residual_grad,
            branch=branch,
            mlp_mid_grad=mlp_mid_grad,
            out_mid_grad=out_mid_grad,
        )
        k["head_grad"] = lax.all_to_all(
            attended_grad.reshape(local_span, shards, own).transpose(1, 0, 2), "shard", 0, 0, tiled=True
        ).reshape(span, own)

    for s in slots:
        k = kept[s]
        keep, give, k["qkv_b"] = attend_back(
            lengths,
            order,
            chips,
            k["q"],
            k["k"],
            k["v"],
            k["lse"],
            k["attended"],
            k["head_grad"],
            k["mids"],
            weight_here,
            k["qkv_map"],
            tables,
            s,
        )
        k["one_sum"] = scatter_hops(keep, give)

    block_parts = []
    token_parts = []
    compact = []
    for s in slots:
        k = kept[s]
        down_mid = k["down_sum"][:, width : width + RANK]
        feed = k["down_sum"][:, :width].astype(jnp.float32) + adapter_scale * dot_nt(
            down_mid, k["down_out"]
        )
        block_parts.append(((k["hidden_in"] + feed) * k["valid"]).astype(low))
        mid_grad = k["one_sum"][:, width : width + 3 * RANK].astype(low)
        normed_grad = k["one_sum"][:, :width] + dot_nt(mid_grad, k["qkv_in"])
        token_parts.append(
            k["residual_grad"]
            + layer_norm_back(normed_grad, k["unit_one"], k["inverse_one"], norm_gain_rows[0])
        )
        compact += [
            dot_tn(mid_grad, k["normed"]),
            dot_tn(k["mlp_mid_grad"], k["normed_two"]),
            dot_tn(k["out_mid_grad"], k["attended_rows"]),
            adapter_scale * dot_tn(k["out_mid"], k["branch"]),
            adapter_scale * dot_tn(down_mid, k["grad_low"]),
        ]
    compact = jnp.concatenate(compact, axis=0).astype(low)
    columns = compact.shape[0]
    owned = scatter_small(compact.reshape(columns, shards, own).transpose(1, 0, 2)).astype(low)
    owned = owned.reshape(slot_count, 8, RANK, own)

    grads = []
    for s in slots:
        k = kept[s]
        part = [owned[s, j] for j in range(8)]
        part += [
            k["qkv_b"][j * RANK : (j + 1) * RANK, j * own : (j + 1) * own].astype(low)
            for j in range(3)
        ]
        part += [
            (adapter_scale * k["g_gate"][:RANK]).astype(low),
            (adapter_scale * k["g_up"][RANK : 2 * RANK]).astype(low),
            k["g_down"][:RANK].astype(low),
        ]
        part += [jnp.broadcast_to(adapters[s].astype(low), (RANK, 128))]
        grads.append(jnp.concatenate(part, axis=1))
    here = jnp.stack(grads)
    reps = lax.axis_size("rep")
    full = 0.0
    for turn in range(reps):
        there = here
        if turn:
            there = lax.ppermute(here, "rep", [(i, (i + turn) % reps) for i in range(reps)])
        for s in slots:
            piece = there[s].astype(jnp.float32)
            index = piece[:, -128:-127][None]
            names = jnp.arange(ADAPTER_COUNT, dtype=jnp.int32).astype(jnp.float32)[:, None, None]
            full = full + jnp.where(index == names, piece[None], 0.0)
    full = full.reshape(ADAPTER_COUNT * RANK, here.shape[2])
    pieces = [full[:, j * own : (j + 1) * own] for j in range(11)]
    rest = [full[:, 11 * own + j * hidden : 11 * own + (j + 1) * hidden] for j in range(3)]
    return (
        jnp.stack(block_parts),
        jnp.stack(token_parts),
        jnp.concatenate([piece.T for piece in pieces[:3]], axis=1),
        jnp.stack(pieces[8:11]),
        pieces[5].T,
        pieces[6],
        jnp.concatenate([piece.T for piece in pieces[3:5]], axis=1),
        jnp.stack([rest[0].T, rest[1].T], axis=1),
        rest[2].T,
        pieces[7],
    )


def solution(mesh):
    rows = P("shard", None)
    in_specs = (
        P("rep", "shard", None),
        P("rep"),
        P("rep"),
        P(),
        P(),
        rows,
        P(),
        rows,
        P("shard", None, None),
        rows,
        rows,
        P(None, None, "shard"),
        rows,
        P(None, "shard"),
        rows,
        P("shard", None, None),
        rows,
        P(None, "shard"),
        P("rep", "shard", None),
    )
    out_specs = (
        P("rep", "shard", None),
        P("rep", "shard", None),
        rows,
        P(None, None, "shard"),
        rows,
        P(None, "shard"),
        rows,
        P("shard", None, None),
        rows,
        P(None, "shard"),
    )
    return jax.shard_map(
        per_device, mesh=mesh, in_specs=in_specs, out_specs=out_specs, check_vma=False
    )
```
